256 devices in a mesh: win: 8 (over x_hi, y), tx: 8 (over z), ty: 4 (over x_lo, core).
Axes of the slice: x: 4 (x_hi: 2, x_lo: 2; x = x_hi * 2 + x_lo), y: 4, z: 8, core: 2. Of those that a mesh axis runs over, the one named last changes fastest.
Arguments:
- dual: float32 [8, 4, 4, 256, 1024], P('win', None, None, 'ty', 'tx'), may hold values from -6 to 6
- obs_dual: float32 [8, 2, 256, 1024], P('win', None, 'ty', 'tx'), may hold values from -6 to 6
- increment: float32 [8, 4, 4, 256, 1024], P('win', None, None, 'ty', 'tx'), may hold values from -6 to 6
- trajectory: float32 [8, 3, 2, 4, 256, 1024], P('win', None, None, None, 'ty', 'tx'), may hold values from -0.3 to 0.3
- diffusion: float32 [4, 4], replicated, may hold values from 0.01 to 0.045
- obs_weight: float32 [2, 4, 4], replicated, may hold values from -1.5 to 1.5
- model_var: float32 [8, 4, 4, 256, 1024], P('win', None, None, 'ty', 'tx'), may hold values from 0.3 to 3
- obs_var: float32 [8, 2, 256, 1024], P('win', None, 'ty', 'tx'), may hold values from 0.5 to 2
Outputs:
- next_dual: float32 [8, 4, 4, 256, 1024], P('win', None, None, 'ty', 'tx')
- next_obs: float32 [8, 2, 256, 1024], P('win', None, 'ty', 'tx')
- next_increment: float32 [8, 4, 4, 256, 1024], P('win', None, None, 'ty', 'tx')
- coeffs: float32 [2], replicated
The draws below stay inside these ranges and needn't reach their ends.
All inputs are finite; a program needn't handle non-finite values.
Results may differ from the reference program's by a relative error of at most 0.00016.
Values sent between devices are 32-bit elements; how exact they have to be, the bound alone decides.
No kernel may reach another device: no remote copies, remote signals or barrier semaphores. Data moves between devices by JAX's collectives and lax.ppermute only.
A program may use at most 128 MiB of HBM per device.

```python
import math
import jax
import jax.numpy as jnp
from jax import lax

F = 4
LEV = 4
STEPS = 3
NOBS = 2
W = 8
NLAT = 256
NLON = 1024


def steps_of(stream_key, shape, pieces, least, high):
    gain, own = 1.0, jax.random.fold_in(stream_key, 6)
    for position, blocks in pieces:
        steps = jnp.exp(jax.random.uniform(jax.random.fold_in(own, position), (blocks,), jnp.float32, least / len(pieces), high / len(pieces)))
        gain = gain * jnp.repeat(steps, shape[position] // blocks).reshape([-1 if axis == position else 1 for axis in range(len(shape))])
    return gain


def normal_values(key, dims, spread, most, split=(), held_as=jnp.bfloat16):
    loudness = steps_of(key, dims, split, -0.22, 0.18) if split else 1.0
    values = jax.random.normal(key, dims, jnp.float32) * spread * loudness
    return jnp.minimum(jnp.maximum(values, -most), most).astype(held_as)


def setup_inputs(seed: int = 0) -> dict:
    key_list = jax.random.split(jax.random.key(seed), 9)
    dual = normal_values(key_list[0], (W, F, LEV, NLAT, NLON), 1.0, 6.0, ((0, 8), (3, 4), (4, 8)), jnp.float32)
    obs_dual = normal_values(key_list[1], (W, NOBS, NLAT, NLON), 1.0, 6.0, ((0, 8), (2, 4), (3, 8)), jnp.float32)
    increment = normal_values(key_list[2], (W, F, LEV, NLAT, NLON), 1.0, 6.0, ((0, 8), (3, 4), (4, 8)), jnp.float32)
    trajectory = jnp.clip(jax.random.uniform(key_list[3], (W, STEPS, 2, LEV, NLAT, NLON), jnp.float32, -0.3, 0.3) * steps_of(key_list[3], (W, STEPS, 2, LEV, NLAT, NLON), ((0, 8), (4, 4), (5, 8)), -0.4, 0.0), -0.3, 0.3)
    diffusion = jnp.clip(jnp.exp(jax.random.uniform(key_list[4], (F, LEV), jnp.float32, math.log(0.01), math.log(0.045))), 0.01, 0.045)
    obs_weight = normal_values(key_list[5], (NOBS, F, LEV), (F * LEV) ** -0.5, 1.5, (), jnp.float32)
    model_var = jnp.clip(jnp.exp(math.log(3.0) - 2.3025851 * jax.random.uniform(key_list[6], (W, F, LEV, NLAT, NLON), jnp.float32) ** steps_of(key_list[6], (W, F, LEV, NLAT, NLON), ((0, 8), (3, 4), (4, 8)), -0.2, 0.2)), 0.3, 3.0)
    obs_var = jnp.clip(jnp.exp(math.log(2.0) - 1.3862944 * jax.random.uniform(key_list[7], (W, NOBS, NLAT, NLON), jnp.float32) ** steps_of(key_list[7], (W, NOBS, NLAT, NLON), ((0, 8), (2, 4), (3, 8)), -0.2, 0.2)), 0.5, 2.0)
    return dict(dual=dual, obs_dual=obs_dual, increment=increment, trajectory=trajectory, diffusion=diffusion, obs_weight=obs_weight, model_var=model_var, obs_var=obs_var)


def neighbours(field):
    east = jnp.roll(field, -1, axis=3)
    west = jnp.roll(field, 1, axis=3)
    zero_row = jnp.zeros_like(field[:, :, :1, :])
    north = jnp.concatenate([field[:, :, 1:, :], zero_row], axis=2)
    south = jnp.concatenate([zero_row, field[:, :, :-1, :]], axis=2)
    return (east, west, north, south)

def forward_step(field, wind_lon, wind_lat, diffuse):
    pos_lon = jnp.maximum(wind_lon, 0.0)[None]
    neg_lon = jnp.minimum(wind_lon, 0.0)[None]
    pos_lat = jnp.maximum(wind_lat, 0.0)[None]
    neg_lat = jnp.minimum(wind_lat, 0.0)[None]
    east, west, north, south = neighbours(field)
    return field - pos_lon * (field - west) - neg_lon * (east - field) - pos_lat * (field - south) - neg_lat * (north - field) + diffuse * (east + west + north + south - 4.0 * field)

def adjoint_step(field, wind_lon, wind_lat, diffuse):
    pos_lon = jnp.maximum(wind_lon, 0.0)[None]
    neg_lon = jnp.minimum(wind_lon, 0.0)[None]
    pos_lat = jnp.maximum(wind_lat, 0.0)[None]
    neg_lat = jnp.minimum(wind_lat, 0.0)[None]
    east, west, north, south = neighbours(field)
    east_pos = jnp.roll(pos_lon * field, -1, axis=3)
    west_neg = jnp.roll(neg_lon * field, 1, axis=3)
    north_pos = neighbours(pos_lat * field)[2]
    south_neg = neighbours(neg_lat * field)[3]
    diagonal = 1.0 - pos_lon + neg_lon - pos_lat + neg_lat - 4.0 * diffuse
    return diagonal * field + east_pos - west_neg + north_pos - south_neg + diffuse * (east + west + north + south)

def reference(dual, obs_dual, increment, trajectory, diffusion, obs_weight, model_var, obs_var):
    diffuse = diffusion[:, :, None, None]
    later_dual = jnp.concatenate([dual[1:], jnp.zeros_like(dual[:1])], axis=0)

    def window(items):
        state, winds, multipliers, following = items
        moved = state
        for index in range(STEPS):
            moved = forward_step(moved, winds[index, 0], winds[index, 1], diffuse)
        obs_end = jnp.einsum('ofl,flab->oab', obs_weight, moved, precision=lax.Precision.HIGHEST)
        adjoint_field = jnp.einsum('ofl,oab->flab', obs_weight, multipliers, precision=lax.Precision.HIGHEST) - following
        for index in reversed(range(STEPS)):
            adjoint_field = adjoint_step(adjoint_field, winds[index, 0], winds[index, 1], diffuse)
        return (moved, obs_end, adjoint_field)
    moved, obs_end, back = lax.map(window, (increment, trajectory, obs_dual, later_dual))
    carried = jnp.concatenate([jnp.zeros_like(moved[:1]), moved[:-1]], axis=0)
    zl = model_var * dual + increment - carried
    zm = obs_var * obs_dual + obs_end
    zd = dual + back
    new_lam = jnp.cumsum(zd[::-1], axis=0)[::-1]
    new_obs = zm / obs_var
    new_state = jnp.cumsum(zl - model_var * new_lam, axis=0)
    inner = jnp.sum(new_lam * dual) + jnp.sum(new_obs * obs_dual) + jnp.sum(new_state * increment)
    square = jnp.sum(dual * dual) + jnp.sum(obs_dual * obs_dual) + jnp.sum(increment * increment)
    coeff = inner / square
    rest_lam = new_lam - coeff * dual
    rest_obs = new_obs - coeff * obs_dual
    rest_state = new_state - coeff * increment
    rest_sq = jnp.sum(rest_lam * rest_lam) + jnp.sum(rest_obs * rest_obs) + jnp.sum(rest_state * rest_state)
    count = dual.size * 2 + obs_dual.size
    scale = jnp.sqrt(rest_sq / count + 1e-06)
    return (rest_lam / scale, rest_obs / scale, rest_state / scale, jnp.stack([coeff, scale]))
```

```python
import functools
import jax
import jax.numpy as jnp
from jax import lax
from jax.experimental import pallas as pl
from jax.experimental.pallas import tpu as pltpu
from jax.sharding import PartitionSpec as P

VM = pl.BlockSpec(memory_space=pltpu.VMEM)
SM = pl.BlockSpec(memory_space=pltpu.SMEM)
HB = pl.BlockSpec(memory_space=pl.ANY)
NF = 16
NW = 24
NO = 2
ALL = NF + NW + NO + NF
PER = 21
ROWS = 64
EXT = ROWS + 16
LANES = 128


def sds(*shape):
    return jax.ShapeDtypeStruct(shape, jnp.float32)


def lanes_of(i):
    lane = lax.broadcasted_iota(jnp.int32, (8, LANES), 1)
    return (lane >= 6 * i) & (lane < 6 * i + 6)


def pack_fields(fetch, count, first):
    acc = jnp.zeros((8, LANES), jnp.float32)
    for i in range(count):
        acc = jnp.where(lanes_of(i), pltpu.roll(fetch(first + i), (6 * i + 3) % LANES, 1), acc)
    return acc


def edges_kernel(inc, winds, obs, dual, top, bottom, packed):
    parts = ((inc, 0, NF), (winds, NF, NW), (obs, NF + NW, NO), (dual, NF + NW + NO, NF))

    def source(f):
        for ref, start, size in parts:
            if f < start + size:
                return ref, f - start

    for ref, start, size in parts:
        top[start : start + size] = ref[:, 0:8, :]
        bottom[start : start + size] = ref[:, ROWS - 8 : ROWS, :]

    def tile(r, carry):
        rows = pl.ds(pl.multiple_of(r * 8, 8), 8)

        def fetch(f):
            ref, at = source(f)
            return ref[at, rows, :]

        for t in range(3):
            count = min(PER, ALL - t * PER)
            packed[rows, t * LANES : (t + 1) * LANES] = pack_fields(fetch, count, t * PER)
        return carry

    lax.fori_loop(0, ROWS // 8, tile, 0)


def edges_halo_kernel(south, north, packed, full):
    full[8 : 8 + ROWS, :] = packed[...]
    for at, ref in ((0, south), (8 + ROWS, north)):
        for t in range(3):
            count = min(PER, ALL - t * PER)
            full[at : at + 8, t * LANES : (t + 1) * LANES] = pack_fields(
                lambda f: ref[f], count, t * PER
            )


def unpack_columns(strip, i):
    return pltpu.roll(strip, (LANES - 3 - 6 * i) % LANES, 1)


def merged(west, east):
    lane = lax.broadcasted_iota(jnp.int32, west.shape, 1) % 6
    return jnp.where(lane < 3, west, east)


def from_sides(x):
    return pltpu.roll(x, 2 * LANES - 1, 1), pltpu.roll(x, 1, 1)


def rows_shifted(ref, f, r, tiles):
    center = ref[f, 8 * r : 8 * r + 8, :]
    if r == 0:
        south = pltpu.roll(center, 1, 0)
    else:
        south = ref[f, 8 * r - 1 : 8 * r + 7, :]
    if r == tiles - 1:
        north = pltpu.roll(center, 7, 0)
    else:
        north = ref[f, 8 * r + 1 : 8 * r + 9, :]
    return center, north, south


TILES = EXT // 8


def load_winds(winds, south, north, west, east, wind):
    for t in range(2):
        strip = merged(
            west[:, t * LANES : (t + 1) * LANES], east[:, t * LANES : (t + 1) * LANES]
        )
        for i in range(PER):
            f = t * PER + i
            if NF <= f < NF + NW:
                wind[f - NF, :, LANES:] = unpack_columns(strip, i)
    wind[:, 0:8, :LANES] = south[NF : NF + NW]
    wind[:, 8 : 8 + ROWS, :LANES] = winds[...]
    wind[:, 8 + ROWS :, :LANES] = north[NF : NF + NW]


def forward_kernel(
    inc, winds, obs, obsvar, south, north, west, east, diffusion, weight, edge,
    late, pm, wind, xa, xb, oacc,
):
    load_winds(winds, south, north, west, east, wind)
    strip = merged(west[:, :LANES], east[:, :LANES])
    for f in range(NF):
        xa[f, :, LANES:] = unpack_columns(strip, f)
    xa[:, 0:8, :LANES] = south[0:NF]
    xa[:, 8 : 8 + ROWS, :LANES] = inc[...]
    xa[:, 8 + ROWS :, :LANES] = north[0:NF]
    oacc[...] = jnp.zeros_like(oacc)
    keep_south = edge[0]
    keep_north = edge[1]
    bufs = (xa, xb)
    for s in range(3):
        src, dst = bufs[s % 2], bufs[(s + 1) % 2]
        last = s == 2

        def level(l, carry, s=s, src=src, dst=dst, last=last):
            for r in range(1, TILES - 1) if last else range(TILES):
                a = wind[s * 8 + l, 8 * r : 8 * r + 8, :]
                b = wind[s * 8 + 4 + l, 8 * r : 8 * r + 8, :]
                pa, na = jnp.maximum(a, 0.0), jnp.minimum(a, 0.0)
                pb, nb = jnp.maximum(b, 0.0), jnp.minimum(b, 0.0)
                base = 1.0 - (pa - na) - (pb - nb)
                sums = [None] * NO
                for f in range(4):
                    k = diffusion[f, l]
                    center, xn, xs = rows_shifted(src, f * 4 + l, r, TILES)
                    xe, xw = from_sides(center)
                    out = (
                        (base - 4.0 * k) * center
                        + (pa + k) * xw
                        + (k - na) * xe
                        + (pb + k) * xs
                        + (k - nb) * xn
                    )
                    if last:
                        out = out[:, :LANES]
                        late[f * 2 + l // 2, l % 2, 8 * r - 8 : 8 * r, :] = out
                        for o in range(NO):
                            term = weight[o, f * 4 + l] * out
                            sums[o] = term if sums[o] is None else sums[o] + term
                    else:
                        if r == 0:
                            out = out * keep_south
                        if r == TILES - 1:
                            out = out * keep_north
                        dst[f * 4 + l, 8 * r : 8 * r + 8, :] = out
                if last:
                    for o in range(NO):
                        oacc[o, 8 * r - 8 : 8 * r, :] += sums[o]
            return carry

        lax.fori_loop(0, 4, level, 0)
    var = obsvar[...]
    pm[...] = (var * obs[...] + oacc[...]) / var


def adjoint_kernel(
    dual, follow, fhalo, winds, obs, south, north, west, east, diffusion, weight, edge,
    late, wind, ya, yb, ob,
):
    load_winds(winds, south, north, west, east, wind)
    strip1 = merged(west[:, LANES : 2 * LANES], east[:, LANES : 2 * LANES])
    for o in range(NO):
        ob[o, :, LANES:] = unpack_columns(strip1, NF + NW + o - PER)
    ob[:, 0:8, :LANES] = south[NF + NW : NF + NW + NO]
    ob[:, 8 : 8 + ROWS, :LANES] = obs[...]
    ob[:, 8 + ROWS :, :LANES] = north[NF + NW : NF + NW + NO]
    for f in range(NF):
        start = weight[0, f] * ob[0] + weight[1, f] * ob[1]
        ya[f, 0:8, :LANES] = start[0:8, :LANES] - fhalo[f]
        ya[f, 8 : 8 + ROWS, :LANES] = start[8 : 8 + ROWS, :LANES] - follow[f]
        ya[f, 8 + ROWS :, :LANES] = start[8 + ROWS :, :LANES] - fhalo[NF + f]
        for r in range(TILES):
            ya[f, 8 * r : 8 * r + 8, LANES:] = start[
                8 * r : 8 * r + 8, LANES:
            ] - unpack_columns(fhalo[2 * NF + r], f)
    keep_south = edge[0]
    keep_north = edge[1]
    bufs = (ya, yb)
    for step in range(3):
        s = 2 - step
        src, dst = bufs[step % 2], bufs[(step + 1) % 2]
        last = step == 2

        def level(l, carry, s=s, src=src, dst=dst, last=last):
            for r in range(1, TILES - 1) if last else range(TILES):
                a = wind[s * 8 + l, 8 * r : 8 * r + 8, :]
                b, bn, bs = rows_shifted(wind, s * 8 + 4 + l, r, TILES)
                pa, na = jnp.maximum(a, 0.0), jnp.minimum(a, 0.0)
                base = 1.0 - (pa - na) - jnp.abs(b)
                pbn = jnp.maximum(bn, 0.0)
                nbs = jnp.minimum(bs, 0.0)
                for f in range(4):
                    k = diffusion[f, l]
                    center, yn, ys = rows_shifted(src, f * 4 + l, r, TILES)
                    east_of, _ = from_sides((pa + k) * center)
                    _, west_of = from_sides((k - na) * center)
                    out = (
                        (base - 4.0 * k) * center
                        + east_of
                        + west_of
                        + (pbn + k) * yn
                        + (k - nbs) * ys
                    )
                    if last:
                        rows = slice(8 * r - 8, 8 * r)
                        late[f * 2 + l // 2, l % 2, rows, :] = (
                            out[:, :LANES] + dual[f * 4 + l, rows, :]
                        )
                    else:
                        if r == 0:
                            out = out * keep_south
                        if r == TILES - 1:
                            out = out * keep_north
                        dst[f * 4 + l, 8 * r : 8 * r + 8, :] = out
            return carry

        lax.fori_loop(0, 4, level, 0)


def scan_kernel(windows, late, early, pm, obs, back, totals, wv, vv, rr):
    wv[...] = jnp.zeros_like(wv)
    vv[...] = jnp.zeros_like(vv)

    def tile(r, carry):
        rows = pl.ds(pl.multiple_of(r * 8, 8), 8)
        for c in range(2):
            run = jnp.zeros((8, LANES), jnp.float32)
            inner = jnp.zeros((8, LANES), jnp.float32)
            square = jnp.zeros((8, LANES), jnp.float32)
            sums = [None] * windows
            for v in reversed(range(windows)):
                run = run + late[v, 2 + c, rows, :]
                sums[v] = run
                back[v, c, rows, :] = run
            run = jnp.zeros((8, LANES), jnp.float32)
            for v in range(windows):
                lam = early[v, c, rows, :]
                inc = early[v, 2 + c, rows, :]
                var = early[v, 4 + c, rows, :]
                term = var * (lam - sums[v]) + inc
                if v:
                    term = term - late[v - 1, c, rows, :]
                run = run + term
                back[v, 2 + c, rows, :] = run
                inner = inner + sums[v] * lam + run * inc
                square = square + lam * lam + inc * inc
            wv[...] += inner
            vv[...] += square
        return carry

    lax.fori_loop(0, ROWS // 8, tile, 0)
    for o in range(NO):
        for r in range(ROWS // 8):
            rows = slice(8 * r, 8 * r + 8)
            x = obs[o, rows, :]
            wv[...] += pm[o, rows, :] * x
            vv[...] += x * x
    inner = jnp.sum(wv[...], keepdims=True)
    square = jnp.sum(vv[...], keepdims=True)
    h = jnp.where(square > 0.0, inner / jnp.where(square > 0.0, square, 1.0), 0.0)
    rr[...] = jnp.zeros_like(rr)

    def rest(r, carry):
        rows = pl.ds(pl.multiple_of(r * 8, 8), 8)
        acc = jnp.zeros((8, LANES), jnp.float32)
        for v in range(windows):
            for c in range(4):
                d = back[v, c, rows, :] - h * early[v, c, rows, :]
                acc = acc + d * d
        for o in range(NO):
            d = pm[o, rows, :] - h * obs[o, rows, :]
            acc = acc + d * d
        rr[...] += acc
        return carry

    lax.fori_loop(0, ROWS // 8, rest, 0)
    remain = jnp.sum(rr[...], keepdims=True)
    lane = lax.broadcasted_iota(jnp.int32, totals.shape, 1)
    totals[...] = jnp.where(
        lane == 0, inner, jnp.where(lane == 1, square, jnp.where(lane == 2, remain, 0.0))
    )


def final_kernel(count, totals, back, dual, inc, pm, obs, o_dual, o_obs, o_inc, coeffs):
    t = totals[...]
    lane = lax.broadcasted_iota(jnp.int32, t.shape, 1)
    inner = jnp.where(lane == 0, t, 0.0)
    square = jnp.where(lane == 0, pltpu.roll(t, LANES - 1, 1), 0.0)
    remain = jnp.where(lane == 0, pltpu.roll(t, LANES - 2, 1), 0.0)
    h_own = jnp.where(square > 0.0, inner / jnp.where(square > 0.0, square, 1.0), 0.0)
    h = jnp.sum(inner, keepdims=True) / jnp.sum(square, keepdims=True)
    d = h - h_own
    uu = jnp.sum(remain + square * d * d, keepdims=True)
    scale = jnp.sqrt(uu / count + 1e-06)
    inv = 1.0 / scale
    first = (lax.broadcasted_iota(jnp.int32, (8, LANES), 0) == 0) & (
        lax.broadcasted_iota(jnp.int32, (8, LANES), 1) == 0
    )
    coeffs[0] = jnp.sum(jnp.where(first, h, 0.0))
    coeffs[1] = jnp.sum(jnp.where(first, scale, 0.0))
    for f in range(NF):
        o_dual[f] = (back[f // 2, f % 2] - h * dual[f]) * inv
        o_inc[f] = (back[f // 2, 2 + f % 2] - h * inc[f]) * inv
    o_obs[...] = (pm[...] - h * obs[...]) * inv


def per_device(dual, obs_dual, increment, trajectory, diffusion, obs_weight, model_var, obs_var):
    windows = lax.axis_size("win")
    columns = lax.axis_size("tx")
    ranks = lax.axis_size("ty")
    lam = dual.reshape(NF, ROWS, LANES)
    inc = increment.reshape(NF, ROWS, LANES)
    winds = trajectory.reshape(NW, ROWS, LANES)
    obs = obs_dual.reshape(NO, ROWS, LANES)
    var = model_var.reshape(NF, ROWS, LANES)
    obsvar = obs_var.reshape(NO, ROWS, LANES)
    weight = obs_weight.reshape(NO, NF)
    row = lax.axis_index("ty")
    edge = jnp.stack([row > 0, row < ranks - 1]).astype(jnp.float32)
    to_previous = [(i + 1, i) for i in range(windows - 1)]

    follow = lax.ppermute(lam, "win", to_previous)
    top, bottom, packed = pl.pallas_call(
        edges_kernel,
        out_shape=(sds(ALL, 8, LANES), sds(ALL, 8, LANES), sds(ROWS, 3 * LANES)),
        in_specs=[VM] * 4,
        out_specs=(VM, VM, VM),
        name="edges",
    )(inc, winds, obs, lam)
    south = lax.ppermute(bottom, "ty", [(i, i + 1) for i in range(ranks - 1)])
    north = lax.ppermute(top, "ty", [(i + 1, i) for i in range(ranks - 1)])
    full = pl.pallas_call(
        edges_halo_kernel,
        out_shape=sds(EXT, 3 * LANES),
        in_specs=[VM] * 3,
        out_specs=VM,
        name="edges_halo",
    )(south, north, packed)
    west = lax.ppermute(full, "tx", [(i, (i + 1) % columns) for i in range(columns)])
    east = lax.ppermute(full, "tx", [((i + 1) % columns, i) for i in range(columns)])

    early = jnp.concatenate(
        [x.reshape(windows, NF // windows, ROWS, LANES) for x in (lam, inc, var)], axis=1
    )
    early = lax.all_to_all(early, "win", 0, 0)

    strip = merged(west[:, 2 * LANES :], east[:, 2 * LANES :])
    fhalo = jnp.concatenate(
        [south[ALL - NF :], north[ALL - NF :], strip.reshape(TILES, 8, LANES)], axis=0
    )
    fhalo = lax.ppermute(fhalo, "win", to_previous)

    field = pltpu.VMEM((NF, EXT, 2 * LANES), jnp.float32)
    wind = pltpu.VMEM((NW, EXT, 2 * LANES), jnp.float32)
    moved, pm = pl.pallas_call(
        forward_kernel,
        out_shape=(sds(windows, NF // windows, ROWS, LANES), sds(NO, ROWS, LANES)),
        in_specs=[VM] * 8 + [SM] * 3,
        out_specs=(VM, VM),
        scratch_shapes=[wind, field, field, pltpu.VMEM((NO, ROWS, LANES), jnp.float32)],
        name="forward",
    )(inc, winds, obs, obsvar, south, north, west, east, diffusion, weight, edge)
    zd = pl.pallas_call(
        adjoint_kernel,
        out_shape=sds(windows, NF // windows, ROWS, LANES),
        in_specs=[VM] * 9 + [SM] * 3,
        out_specs=VM,
        scratch_shapes=[wind, field, field, pltpu.VMEM((NO, EXT, 2 * LANES), jnp.float32)],
        name="adjoint",
    )(lam, follow, fhalo, winds, obs, south, north, west, east, diffusion, weight, edge)

    late = lax.all_to_all(jnp.concatenate([moved, zd], axis=1), "win", 0, 0)
    devices = windows * columns * ranks
    tile = pltpu.VMEM((8, LANES), jnp.float32)
    back, totals = pl.pallas_call(
        functools.partial(scan_kernel, windows),
        out_shape=(sds(windows, 4, ROWS, LANES), sds(devices, LANES)),
        in_specs=[VM] * 4,
        out_specs=(VM, VM),
        scratch_shapes=[tile, tile, tile],
        name="scans",
    )(late, early, pm, obs)
    totals = lax.all_to_all(totals, ("win", "tx", "ty"), 0, 0)
    back = lax.all_to_all(back, "win", 0, 0)

    count = float((2 * NF + NO) * ROWS * LANES * devices)
    o_dual, o_obs, o_inc, coeffs = pl.pallas_call(
        functools.partial(final_kernel, count),
        out_shape=(sds(NF, ROWS, LANES), sds(NO, ROWS, LANES), sds(NF, ROWS, LANES), sds(2)),
        in_specs=[VM] * 6,
        out_specs=(VM, VM, VM, SM),
        name="final",
    )(totals, back, lam, inc, pm, obs)
    return (
        o_dual.reshape(dual.shape),
        o_obs.reshape(obs_dual.shape),
        o_inc.reshape(increment.shape),
        coeffs,
    )


def solution(mesh):
    in_specs = (
        P("win", None, None, "ty", "tx"),
        P("win", None, "ty", "tx"),
        P("win", None, None, "ty", "tx"),
        P("win", None, None, None, "ty", "tx"),
        P(),
        P(),
        P("win", None, None, "ty", "tx"),
        P("win", None, "ty", "tx"),
    )
    out_specs = (
        P("win", None, None, "ty", "tx"),
        P("win", None, "ty", "tx"),
        P("win", None, None, "ty", "tx"),
        P(),
    )
    return jax.shard_map(
        per_device, mesh=mesh, in_specs=in_specs, out_specs=out_specs, check_vma=False
    )
```

```python
import functools
import jax
import jax.numpy as jnp
from jax import lax
from jax.experimental import pallas as pl
from jax.experimental.pallas import tpu as pltpu
from jax.sharding import PartitionSpec as P

VM = pl.BlockSpec(memory_space=pltpu.VMEM)
SM = pl.BlockSpec(memory_space=pltpu.SMEM)
HB = pl.BlockSpec(memory_space=pl.ANY)
NF = 16
NW = 24
NO = 2
ALL = NF + NF + NW + NO
D0, X0, W0, O0 = 0, NF, 2 * NF, 2 * NF + NW
PER = 21
GROUPS = ((D0, NF), (X0, PER), (X0 + PER, PER))
ROWS = 64
EXT = ROWS + 16
LANES = 128
GRANT = pltpu.CompilerParams(vmem_limit_bytes=16 * 1024 * 1024)


def sds(*shape):
    return jax.ShapeDtypeStruct(shape, jnp.float32)


def vmem(*shape):
    return pltpu.VMEM(shape, jnp.float32)


def far(x):
    return pltpu.with_memory_space_constraint(x, pltpu.HBM)


def held(x):
    return pltpu.with_memory_space_constraint(x, pltpu.VMEM)


def lanes_of(i):
    lane = lax.broadcasted_iota(jnp.int32, (8, LANES), 1)
    return (lane >= 6 * i) & (lane < 6 * i + 6)


def pack_fields(fetch, count, first):
    acc = jnp.zeros((8, LANES), jnp.float32)
    for i in range(count):
        acc = jnp.where(lanes_of(i), pltpu.roll(fetch(first + i), (6 * i + 3) % LANES, 1), acc)
    return acc


def edges_kernel(*refs):
    tops, bottoms, (top, bottom) = refs[0:4], refs[4:8], refs[8:]
    start = 0
    for a, b in zip(tops, bottoms):
        size = a.shape[0]
        top[start : start + size] = a[...]
        bottom[start : start + size] = b[...]
        start += size
    top[0, 7:8, :] = jnp.ones((1, LANES), jnp.float32)
    bottom[0, 0:1, :] = jnp.ones((1, LANES), jnp.float32)


def pack_kernel(dual, inc, winds, obs, packed):
    parts = ((dual, D0, NF), (inc, X0, NF), (winds, W0, NW), (obs, O0, NO))

    def tile(r, carry):
        rows = pl.ds(pl.multiple_of(r * 8, 8), 8)

        def fetch(f):
            for ref, start, size in parts:
                if f < start + size:
                    return ref[f - start, rows, :]

        for t, (first, count) in enumerate(GROUPS):
            packed[rows, t * LANES : (t + 1) * LANES] = pack_fields(fetch, count, first)
        return carry

    lax.fori_loop(0, ROWS // 8, tile, 0)


def edges_halo_kernel(south, north, packed, full):
    full[8 : 8 + ROWS, :] = packed[...]
    for at, ref in ((0, south), (8 + ROWS, north)):
        for t, (first, count) in enumerate(GROUPS):
            full[at : at + 8, t * LANES : (t + 1) * LANES] = pack_fields(
                lambda f: ref[f], count, first
            )


def follow_halo_kernel(south, north, west, east, out):
    out[0:NF] = south[0:NF]
    out[NF : 2 * NF] = north[0:NF]
    for r in range(TILES):
        rows = slice(8 * r, 8 * r + 8)
        out[2 * NF + r] = merged(west[rows, 0:LANES], east[rows, 0:LANES])


def unpack_columns(strip, i):
    return pltpu.roll(strip, (LANES - 3 - 6 * i) % LANES, 1)


def merged(west, east):
    lane = lax.broadcasted_iota(jnp.int32, west.shape, 1) % 6
    return jnp.where(lane < 3, west, east)


def from_sides(x):
    return pltpu.roll(x, 2 * LANES - 1, 1), pltpu.roll(x, 1, 1)


def rows_shifted(ref, f, r, tiles):
    center = ref[f, 8 * r : 8 * r + 8, :]
    if r == 0:
        south = pltpu.roll(center, 1, 0)
    else:
        south = ref[f, 8 * r - 1 : 8 * r + 7, :]
    if r == tiles - 1:
        north = pltpu.roll(center, 7, 0)
    else:
        north = ref[f, 8 * r + 1 : 8 * r + 9, :]
    return center, north, south


TILES = EXT // 8


def strip_of(west, east, t):
    lanes = slice((t + 1) * LANES, (t + 2) * LANES)
    return merged(west[:, lanes], east[:, lanes])


def load_field(ref, at, f, rows, south, north, strips):
    ref[at, 0:8, :LANES] = south[f]
    ref[at, 8 : 8 + ROWS, :LANES] = rows
    ref[at, 8 + ROWS :, :LANES] = north[f]
    place = f - X0
    ref[at, :, LANES:] = unpack_columns(strips[place // PER], place % PER)


def load_winds(winds, south, north, strips, wind):
    for i in range(NW):
        load_field(wind, i, W0 + i, winds[i], south, north, strips)


def forward_kernel(
    inc, dual, var, winds, obs, obsvar, south, north, west, east, diffusion, weight,
    late, moved, pm, wind, xa, xb, oacc,
):
    strips = [strip_of(west, east, t) for t in range(2)]
    load_winds(winds, south, north, strips, wind)
    for f in range(NF):
        load_field(xa, f, X0 + f, inc[f], south, north, strips)
    oacc[...] = jnp.zeros_like(oacc)
    keep_south = south[D0, 0:1, 0:1]
    keep_north = north[D0, 7:8, 0:1]
    bufs = (xa, xb)
    for s in range(3):
        src, dst = bufs[s % 2], bufs[(s + 1) % 2]
        last = s == 2

        def level(l, carry, s=s, src=src, dst=dst, last=last):
            for r in range(1, TILES - 1) if last else range(TILES):
                a = wind[s * 8 + l, 8 * r : 8 * r + 8, :]
                b = wind[s * 8 + 4 + l, 8 * r : 8 * r + 8, :]
                pa, na = jnp.maximum(a, 0.0), jnp.minimum(a, 0.0)
                pb, nb = jnp.maximum(b, 0.0), jnp.minimum(b, 0.0)
                base = 1.0 - (pa - na) - (pb - nb)
                sums = [None] * NO
                for f in range(4):
                    k = diffusion[f, l]
                    center, xn, xs = rows_shifted(src, f * 4 + l, r, TILES)
                    xe, xw = from_sides(center)
                    out = (
                        (base - 4.0 * k) * center
                        + (pa + k) * xw
                        + (k - na) * xe
                        + (pb + k) * xs
                        + (k - nb) * xn
                    )
                    if last:
                        out = out[:, :LANES]
                        n = f * 4 + l
                        rows = slice(8 * r - 8, 8 * r)
                        moved[n, rows, :] = out
                        late[f * 2 + l // 2, l % 2, rows, :] = (
                            var[n, rows, :] * dual[n, rows, :] + inc[n, rows, :] - out
                        )
                        for o in range(NO):
                            term = weight[o, f, l] * out
                            sums[o] = term if sums[o] is None else sums[o] + term
                    else:
                        if r == 0:
                            out = out * keep_south
                        if r == TILES - 1:
                            out = out * keep_north
                        dst[f * 4 + l, 8 * r : 8 * r + 8, :] = out
                if last:
                    for o in range(NO):
                        oacc[o, 8 * r - 8 : 8 * r, :] += sums[o]
            return carry

        lax.fori_loop(0, 4, level, 0)
    for n in range(NF):
        late[n // 2, 4 + n % 2] = var[n]
    spread = obsvar[...]
    pm[...] = (spread * obs[...] + oacc[...]) / spread


def adjoint_kernel(
    late_in, dual, follow, fhalo, winds, obs, south, north, west, east, diffusion, weight,
    late, wind, ya, yb, ob,
):
    strips = [strip_of(west, east, t) for t in range(2)]
    load_winds(winds, south, north, strips, wind)
    for o in range(NO):
        load_field(ob, o, O0 + o, obs[o], south, north, strips)
    for f in range(NF):
        start = weight[0, f // 4, f % 4] * ob[0] + weight[1, f // 4, f % 4] * ob[1]
        ya[f, 0:8, :LANES] = start[0:8, :LANES] - fhalo[f]
        ya[f, 8 : 8 + ROWS, :LANES] = start[8 : 8 + ROWS, :LANES] - follow[f]
        ya[f, 8 + ROWS :, :LANES] = start[8 + ROWS :, :LANES] - fhalo[NF + f]
        for r in range(TILES):
            ya[f, 8 * r : 8 * r + 8, LANES:] = start[
                8 * r : 8 * r + 8, LANES:
            ] - unpack_columns(fhalo[2 * NF + r], f)
    keep_south = south[D0, 0:1, 0:1]
    keep_north = north[D0, 7:8, 0:1]
    bufs = (ya, yb)
    for step in range(3):
        s = 2 - step
        src, dst = bufs[step % 2], bufs[(step + 1) % 2]
        last = step == 2

        def level(l, carry, s=s, src=src, dst=dst, last=last):
            for r in range(1, TILES - 1) if last else range(TILES):
                a = wind[s * 8 + l, 8 * r : 8 * r + 8, :]
                b, bn, bs = rows_shifted(wind, s * 8 + 4 + l, r, TILES)
                pa, na = jnp.maximum(a, 0.0), jnp.minimum(a, 0.0)
                base = 1.0 - (pa - na) - jnp.abs(b)
                pbn = jnp.maximum(bn, 0.0)
                nbs = jnp.minimum(bs, 0.0)
                for f in range(4):
                    k = diffusion[f, l]
                    center, yn, ys = rows_shifted(src, f * 4 + l, r, TILES)
                    east_of, _ = from_sides((pa + k) * center)
                    _, west_of = from_sides((k - na) * center)
                    out = (
                        (base - 4.0 * k) * center
                        + east_of
                        + west_of
                        + (pbn + k) * yn
                        + (k - nbs) * ys
                    )
                    if last:
                        rows = slice(8 * r - 8, 8 * r)
                        late[f * 2 + l // 2, 2 + l % 2, rows, :] = (
                            out[:, :LANES] + dual[f * 4 + l, rows, :]
                        )
                    else:
                        if r == 0:
                            out = out * keep_south
                        if r == TILES - 1:
                            out = out * keep_north
                        dst[f * 4 + l, 8 * r : 8 * r + 8, :] = out
            return carry

        lax.fori_loop(0, 4, level, 0)


def ratio(inner, square):
    live = square > 0.0
    return jnp.where(live, inner / jnp.where(live, square, 1.0), 0.0)


def total_of(x):
    return jnp.sum(x, keepdims=True)


def share(inner, square, remain):
    lane = lax.broadcasted_iota(jnp.int32, (8, LANES), 1)
    return jnp.where(
        lane == 0, inner, jnp.where(lane == 1, square, jnp.where(lane == 2, remain, 0.0))
    )


def combine(t):
    lane = lax.broadcasted_iota(jnp.int32, t.shape, 1) == 0
    inner = jnp.where(lane, t, 0.0)
    square = jnp.where(lane, pltpu.roll(t, LANES - 1, 1), 0.0)
    remain = jnp.where(lane, pltpu.roll(t, LANES - 2, 1), 0.0)
    inner_sum, square_sum = total_of(inner), total_of(square)
    d = ratio(inner_sum, square_sum) - ratio(inner, square)
    return inner_sum, square_sum, total_of(remain + square * d * d)


def scan_kernel(windows, late, back):
    def tile(r, carry):
        rows = pl.ds(pl.multiple_of(r * 8, 8), 8)
        for c in range(2):
            run = jnp.zeros((8, LANES), jnp.float32)
            sums = [None] * windows
            for v in reversed(range(windows)):
                run = run + late[v, 2 + c, rows, :]
                sums[v] = run
                back[v, c, rows, :] = run
            run = jnp.zeros((8, LANES), jnp.float32)
            for v in range(windows):
                run = run + (late[v, c, rows, :] - late[v, 4 + c, rows, :] * sums[v])
                back[v, 2 + c, rows, :] = run
        return carry

    lax.fori_loop(0, ROWS // 8, tile, 0)


def dots_kernel(back, moved, dual, inc, pm, obs, shares, px, wv, vv, rr):
    windows = back.shape[0]
    per = NF // windows
    rr[...] = jnp.zeros_like(rr)

    def tile(r, carry):
        rows = pl.ds(pl.multiple_of(r * 8, 8), 8)
        total = jnp.zeros((8, LANES), jnp.float32)
        for half in range(2):
            pairs = [(pm[half, rows, :], obs[half, rows, :])]
            for f in range(half * NF // 2, (half + 1) * NF // 2):
                j, c = f // per, f % per
                x = back[j, per + c, rows, :] + moved[f, rows, :]
                px[f, rows, :] = x
                pairs.append((back[j, c, rows, :], dual[f, rows, :]))
                pairs.append((x, inc[f, rows, :]))
            inner = functools.reduce(jnp.add, [p * x for p, x in pairs])
            square = functools.reduce(jnp.add, [x * x for _, x in pairs])
            h = ratio(inner, square)
            for p, x in pairs:
                d = p - h * x
                total = total + d * d
            wv[2 * r + half] = inner
            vv[2 * r + half] = square
        rr[...] += total
        return carry

    lax.fori_loop(0, ROWS // 8, tile, 0)
    inner, square = wv[...], vv[...]
    h = ratio(inner, square)
    inner_sum = total_of(jnp.sum(inner, 0))
    square_sum = total_of(jnp.sum(square, 0))
    d = ratio(inner_sum, square_sum) - h
    remain = total_of(rr[...] + jnp.sum(square * d * d, 0))
    one = share(inner_sum, square_sum, remain)
    for r in range(shares.shape[0] // 8):
        shares[8 * r : 8 * r + 8, :] = one


def final_kernel(
    count, shares, back, px, dual, inc, pm, obs, o_dual, o_obs, o_inc, coeffs, dv, iv, sems
):
    windows = back.shape[0]
    per = NF // windows
    inner, square, remain = combine(shares[...])
    h = inner / square
    scale = jnp.sqrt(remain / count + 1e-06)
    inv = 1.0 / scale
    first = (lax.broadcasted_iota(jnp.int32, (8, LANES), 0) == 0) & (
        lax.broadcasted_iota(jnp.int32, (8, LANES), 1) == 0
    )
    coeffs[0] = jnp.sum(jnp.where(first, h, 0.0))
    coeffs[1] = jnp.sum(jnp.where(first, scale, 0.0))
    o_obs[...] = (pm[...] - h * obs[...]) * inv
    stores = []
    for n in range(4):
        for f in range(4 * n, 4 * n + 4):
            dv[f] = (back[f // per, f % per] - h * dual[f]) * inv
            iv[f] = (px[f] - h * inc[f]) * inv
        part = slice(4 * n, 4 * n + 4)
        for m, (src, dst) in enumerate(((dv, o_dual), (iv, o_inc))):
            copy = pltpu.make_async_copy(src.at[part], dst.at[part], sems.at[n, m])
            copy.start()
            stores.append(copy)
    for copy in stores:
        copy.wait()


def dma(*shape):
    return pltpu.SemaphoreType.DMA(shape)


def block(*shape, at):
    return pl.BlockSpec(shape, lambda i: at)


def across(x, axes):
    return lax.all_to_all(x, axes, 0, 0, tiled=True)


def iteration(dual, obs_dual, increment, trajectory, diffusion, obs_weight, model_var, obs_var):
    windows = lax.axis_size("win")
    columns = lax.axis_size("tx")
    ranks = lax.axis_size("ty")
    devices = windows * columns * ranks
    per = NF // windows
    tied = lax.optimization_barrier
    lam = dual.reshape(NF, ROWS, LANES)
    inc = increment.reshape(NF, ROWS, LANES)
    winds = trajectory.reshape(NW, ROWS, LANES)
    obs = obs_dual.reshape(NO, ROWS, LANES)
    var = model_var.reshape(NF, ROWS, LANES)
    obsvar = obs_var.reshape(NO, ROWS, LANES)
    to_previous = [(i + 1, i) for i in range(windows - 1)]

    every = (lam, inc, winds, obs)
    last = ROWS // 8 - 1
    top, bottom = pl.pallas_call(
        edges_kernel,
        grid=(1,),
        out_shape=(vmem(ALL, 8, LANES), vmem(ALL, 8, LANES)),
        in_specs=[block(x.shape[0], 8, LANES, at=(0, 0, 0)) for x in every]
        + [block(x.shape[0], 8, LANES, at=(0, last, 0)) for x in every],
        out_specs=[VM, VM],
        compiler_params=GRANT,
        name="edges",
    )(*(far(x) for x in every + every))
    south = held(lax.ppermute(bottom, "ty", [(i, i + 1) for i in range(ranks - 1)]))
    north = held(lax.ppermute(top, "ty", [(i + 1, i) for i in range(ranks - 1)]))
    packed = pl.pallas_call(
        pack_kernel,
        out_shape=vmem(ROWS, 3 * LANES),
        in_specs=[VM] * 4,
        out_specs=VM,
        compiler_params=GRANT,
        name="pack",
    )(*(held(x) for x in every))
    full = pl.pallas_call(
        edges_halo_kernel,
        out_shape=vmem(EXT, 3 * LANES),
        in_specs=[VM] * 3,
        out_specs=VM,
        compiler_params=GRANT,
        name="edges_halo",
    )(south, north, packed)
    full, lam_out = tied((full, lam))
    ring = [(i, (i + 1) % columns) for i in range(columns)]
    west = held(lax.ppermute(full, "tx", ring))
    east = held(lax.ppermute(full, "tx", [(j, i) for i, j in ring]))
    follow = held(lax.ppermute(lam_out, "win", to_previous))

    fhalo = pl.pallas_call(
        follow_halo_kernel,
        out_shape=vmem(2 * NF + TILES, 8, LANES),
        in_specs=[VM] * 4,
        out_specs=VM,
        compiler_params=GRANT,
        name="follow_halo",
    )(south, north, west, east)
    fhalo = held(lax.ppermute(fhalo, "win", to_previous))

    field = vmem(NF, EXT, 2 * LANES)
    wind = vmem(NW, EXT, 2 * LANES)
    late, moved, pm = pl.pallas_call(
        forward_kernel,
        out_shape=(
            vmem(windows, 3 * per, ROWS, LANES),
            vmem(NF, ROWS, LANES),
            vmem(NO, ROWS, LANES),
        ),
        in_specs=[VM] * 10 + [SM] * 2,
        out_specs=(VM, VM, VM),
        scratch_shapes=[wind, field, field, vmem(NO, ROWS, LANES)],
        compiler_params=GRANT,
        name="forward",
    )(held(inc), held(lam), held(var), held(winds), held(obs), held(obsvar), south, north, west, east, diffusion, obs_weight)
    late = pl.pallas_call(
        adjoint_kernel,
        out_shape=vmem(windows, 3 * per, ROWS, LANES),
        in_specs=[VM] * 10 + [SM] * 2,
        out_specs=VM,
        scratch_shapes=[wind, field, field, vmem(NO, EXT, 2 * LANES)],
        input_output_aliases={0: 0},
        compiler_params=GRANT,
        name="adjoint",
    )(late, held(lam), follow, fhalo, held(winds), held(obs), south, north, west, east, diffusion, obs_weight)

    late = held(across(late, "win"))
    tiles = 2 * ROWS // 8
    back = pl.pallas_call(
        functools.partial(scan_kernel, windows),
        out_shape=vmem(windows, 2 * per, ROWS, LANES),
        in_specs=[VM],
        out_specs=VM,
        compiler_params=GRANT,
        name="scans",
    )(late)
    back = held(across(back, "win"))
    shares, px = pl.pallas_call(
        dots_kernel,
        out_shape=(vmem(devices, LANES), vmem(NF, ROWS, LANES)),
        in_specs=[VM] * 6,
        out_specs=(VM, VM),
        scratch_shapes=[vmem(tiles, 8, LANES), vmem(tiles, 8, LANES), vmem(8, LANES)],
        compiler_params=GRANT,
        name="dots",
    )(back, moved, held(lam), held(inc), pm, held(obs))
    shares = across(shares, ("win", "tx", "ty"))
    count = float((2 * NF + NO) * ROWS * LANES * devices)
    o_dual, o_obs, o_inc, coeffs = pl.pallas_call(
        functools.partial(final_kernel, count),
        out_shape=(sds(NF, ROWS, LANES), sds(NO, ROWS, LANES), sds(NF, ROWS, LANES), sds(2)),
        in_specs=[VM] * 7,
        out_specs=(HB, VM, HB, SM),
        scratch_shapes=[vmem(NF, ROWS, LANES), vmem(NF, ROWS, LANES), dma(4, 2)],
        compiler_params=GRANT,
        name="final",
    )(held(shares), back, px, held(lam), held(inc), pm, held(obs))
    return (
        o_dual.reshape(dual.shape),
        o_obs.reshape(obs_dual.shape),
        o_inc.reshape(increment.shape),
        coeffs,
    )


def solution(mesh):
    in_specs = (
        P("win", None, None, "ty", "tx"),
        P("win", None, "ty", "tx"),
        P("win", None, None, "ty", "tx"),
        P("win", None, None, None, "ty", "tx"),
        P(),
        P(),
        P("win", None, None, "ty", "tx"),
        P("win", None, "ty", "tx"),
    )
    out_specs = (
        P("win", None, None, "ty", "tx"),
        P("win", None, "ty", "tx"),
        P("win", None, None, "ty", "tx"),
        P(),
    )
    return jax.shard_map(
        iteration, mesh=mesh, in_specs=in_specs, out_specs=out_specs, check_vma=False
    )
```

```python
import functools
import jax
import jax.numpy as jnp
from jax import lax
from jax.experimental import pallas as pl
from jax.experimental.pallas import tpu as pltpu
from jax.sharding import PartitionSpec as P

VM = pl.BlockSpec(memory_space=pltpu.VMEM)
SM = pl.BlockSpec(memory_space=pltpu.SMEM)
HB = pl.BlockSpec(memory_space=pl.ANY)
NF = 16
NW = 24
NO = 2
ALL = NF + NF + NW + NO
D0, X0, W0, O0 = 0, NF, 2 * NF, 2 * NF + NW
PER = 21
GROUPS = ((D0, NF), (X0, PER), (X0 + PER, PER))
ROWS = 64
EXT = ROWS + 16
LANES = 128
GRANT = pltpu.CompilerParams(vmem_limit_bytes=16 * 1024 * 1024)


def sds(*shape):
    return jax.ShapeDtypeStruct(shape, jnp.float32)


def vmem(*shape):
    return pltpu.VMEM(shape, jnp.float32)


def far(x):
    return pltpu.with_memory_space_constraint(x, pltpu.HBM)


def held(x):
    return pltpu.with_memory_space_constraint(x, pltpu.VMEM)


def lanes_of(i):
    lane = lax.broadcasted_iota(jnp.int32, (8, LANES), 1)
    return (lane >= 6 * i) & (lane < 6 * i + 6)


def pack_fields(fetch, count, first):
    acc = jnp.zeros((8, LANES), jnp.float32)
    for i in range(count):
        acc = jnp.where(lanes_of(i), pltpu.roll(fetch(first + i), (6 * i + 3) % LANES, 1), acc)
    return acc


def down(x, rows):
    return pltpu.roll(x, rows % 8, 0)


def edges_kernel(*refs):
    tops, bottoms, (top, bottom) = refs[0:4], refs[4:8], refs[8:]
    upper = lax.broadcasted_iota(jnp.int32, (8, LANES), 0) < 4
    start = 0
    for a, b in zip(tops, bottoms):
        for p in range(a.shape[0] // 2):
            top[start + p] = jnp.where(upper, a[2 * p], down(a[2 * p + 1], 4))
            bottom[start + p] = jnp.where(upper, down(b[2 * p], 3), down(b[2 * p + 1], -1))
        start += a.shape[0] // 2
    for ref in (top, bottom):
        ref[0, 3:4, :] = jnp.ones((1, LANES), jnp.float32)


def south_tile(ref, f):
    return down(ref[f // 2], 1 if f % 2 else 5)


def north_tile(ref, f):
    return down(ref[f // 2], 4) if f % 2 else ref[f // 2]


def pack_kernel(dual, inc, winds, obs, packed):
    parts = ((dual, D0, NF), (inc, X0, NF), (winds, W0, NW), (obs, O0, NO))

    def tile(r, carry):
        rows = pl.ds(pl.multiple_of(r * 8, 8), 8)

        def fetch(f):
            for ref, start, size in parts:
                if f < start + size:
                    return ref[f - start, rows, :]

        for t, (first, count) in enumerate(GROUPS):
            packed[rows, t * LANES : (t + 1) * LANES] = pack_fields(fetch, count, first)
        return carry

    lax.fori_loop(0, ROWS // 8, tile, 0)


def edges_halo_kernel(south, north, packed, full):
    full[8 : 8 + ROWS, :] = packed[...]
    for at, tile_of, ref in ((0, south_tile, south), (8 + ROWS, north_tile, north)):
        for t, (first, count) in enumerate(GROUPS):
            full[at : at + 8, t * LANES : (t + 1) * LANES] = pack_fields(
                functools.partial(tile_of, ref), count, first
            )


def follow_halo_kernel(south, north, west, east, out):
    half = NF // 2
    out[0:half] = south[0:half]
    out[half:NF] = north[0:half]
    for r in range(TILES):
        rows = slice(8 * r, 8 * r + 8)
        out[NF + r] = merged(west[rows, 0:LANES], east[rows, 0:LANES])


def unpack_columns(strip, i):
    return pltpu.roll(strip, (LANES - 3 - 6 * i) % LANES, 1)


def merged(west, east):
    lane = lax.broadcasted_iota(jnp.int32, west.shape, 1) % 6
    return jnp.where(lane < 3, west, east)


def from_sides(x):
    return pltpu.roll(x, 2 * LANES - 1, 1), pltpu.roll(x, 1, 1)


def rows_shifted(ref, f, r, tiles):
    center = ref[f, 8 * r : 8 * r + 8, :]
    if r == 0:
        south = pltpu.roll(center, 1, 0)
    else:
        south = ref[f, 8 * r - 1 : 8 * r + 7, :]
    if r == tiles - 1:
        north = pltpu.roll(center, 7, 0)
    else:
        north = ref[f, 8 * r + 1 : 8 * r + 9, :]
    return center, north, south


TILES = EXT // 8


def strip_of(west, east, t):
    lanes = slice((t + 1) * LANES, (t + 2) * LANES)
    return merged(west[:, lanes], east[:, lanes])


def load_field(ref, at, f, rows, south, north, strips):
    ref[at, 0:8, :LANES] = south_tile(south, f)
    ref[at, 8 : 8 + ROWS, :LANES] = rows
    ref[at, 8 + ROWS :, :LANES] = north_tile(north, f)
    place = f - X0
    ref[at, :, LANES:] = unpack_columns(strips[place // PER], place % PER)


def load_winds(winds, south, north, strips, wind):
    for i in range(NW):
        load_field(wind, i, W0 + i, winds[i], south, north, strips)


def forward_kernel(
    inc, dual, var, winds, obs, obsvar, south, north, west, east, diffusion, weight,
    late, moved, pm, wind, xa, xb, oacc,
):
    strips = [strip_of(west, east, t) for t in range(2)]
    load_winds(winds, south, north, strips, wind)
    for f in range(NF):
        load_field(xa, f, X0 + f, inc[f], south, north, strips)
    oacc[...] = jnp.zeros_like(oacc)
    keep_south = south[0, 3:4, 0:1]
    keep_north = north[0, 3:4, 0:1]
    bufs = (xa, xb)
    for s in range(3):
        src, dst = bufs[s % 2], bufs[(s + 1) % 2]
        last = s == 2

        def level(l, carry, s=s, src=src, dst=dst, last=last):
            for r in range(1, TILES - 1) if last else range(TILES):
                a = wind[s * 8 + l, 8 * r : 8 * r + 8, :]
                b = wind[s * 8 + 4 + l, 8 * r : 8 * r + 8, :]
                pa, na = jnp.maximum(a, 0.0), jnp.minimum(a, 0.0)
                pb, nb = jnp.maximum(b, 0.0), jnp.minimum(b, 0.0)
                base = 1.0 - (pa - na) - (pb - nb)
                sums = [None] * NO
                for f in range(4):
                    k = diffusion[f, l]
                    center, xn, xs = rows_shifted(src, f * 4 + l, r, TILES)
                    xe, xw = from_sides(center)
                    out = (
                        (base - 4.0 * k) * center
                        + (pa + k) * xw
                        + (k - na) * xe
                        + (pb + k) * xs
                        + (k - nb) * xn
                    )
                    if last:
                        out = out[:, :LANES]
                        n = f * 4 + l
                        rows = slice(8 * r - 8, 8 * r)
                        moved[n, rows, :] = out
                        late[f * 2 + l // 2, l % 2, rows, :] = (
                            var[n, rows, :] * dual[n, rows, :] + inc[n, rows, :] - out
                        )
                        for o in range(NO):
                            term = weight[o, f, l] * out
                            sums[o] = term if sums[o] is None else sums[o] + term
                    else:
                        if r == 0:
                            out = out * keep_south
                        if r == TILES - 1:
                            out = out * keep_north
                        dst[f * 4 + l, 8 * r : 8 * r + 8, :] = out
                if last:
                    for o in range(NO):
                        oacc[o, 8 * r - 8 : 8 * r, :] += sums[o]
            return carry

        lax.fori_loop(0, 4, level, 0)
    for n in range(NF):
        late[n // 2, 4 + n % 2] = var[n]
    spread = obsvar[...]
    pm[...] = (spread * obs[...] + oacc[...]) / spread


def adjoint_kernel(
    late_in, dual, follow, fhalo, wind, obs, south, north, west, east, diffusion, weight,
    late, ya, yb, ob,
):
    strips = [strip_of(west, east, t) for t in range(2)]
    for o in range(NO):
        load_field(ob, o, O0 + o, obs[o], south, north, strips)
    for f in range(NF):
        start = weight[0, f // 4, f % 4] * ob[0] + weight[1, f // 4, f % 4] * ob[1]
        ya[f, 0:8, :LANES] = start[0:8, :LANES] - south_tile(fhalo, f)
        ya[f, 8 : 8 + ROWS, :LANES] = start[8 : 8 + ROWS, :LANES] - follow[f]
        ya[f, 8 + ROWS :, :LANES] = start[8 + ROWS :, :LANES] - north_tile(fhalo, NF + f)
        for r in range(TILES):
            ya[f, 8 * r : 8 * r + 8, LANES:] = start[
                8 * r : 8 * r + 8, LANES:
            ] - unpack_columns(fhalo[NF + r], f)
    keep_south = south[0, 3:4, 0:1]
    keep_north = north[0, 3:4, 0:1]
    bufs = (ya, yb)
    for step in range(3):
        s = 2 - step
        src, dst = bufs[step % 2], bufs[(step + 1) % 2]
        last = step == 2

        def level(l, carry, s=s, src=src, dst=dst, last=last):
            for r in range(1, TILES - 1) if last else range(TILES):
                a = wind[s * 8 + l, 8 * r : 8 * r + 8, :]
                b, bn, bs = rows_shifted(wind, s * 8 + 4 + l, r, TILES)
                pa, na = jnp.maximum(a, 0.0), jnp.minimum(a, 0.0)
                base = 1.0 - (pa - na) - jnp.abs(b)
                pbn = jnp.maximum(bn, 0.0)
                nbs = jnp.minimum(bs, 0.0)
                for f in range(4):
                    k = diffusion[f, l]
                    center, yn, ys = rows_shifted(src, f * 4 + l, r, TILES)
                    east_of, _ = from_sides((pa + k) * center)
                    _, west_of = from_sides((k - na) * center)
                    out = (
                        (base - 4.0 * k) * center
                        + east_of
                        + west_of
                        + (pbn + k) * yn
                        + (k - nbs) * ys
                    )
                    if last:
                        rows = slice(8 * r - 8, 8 * r)
                        late[f * 2 + l // 2, 2 + l % 2, rows, :] = (
                            out[:, :LANES] + dual[f * 4 + l, rows, :]
                        )
                    else:
                        if r == 0:
                            out = out * keep_south
                        if r == TILES - 1:
                            out = out * keep_north
                        dst[f * 4 + l, 8 * r : 8 * r + 8, :] = out
            return carry

        lax.fori_loop(0, 4, level, 0)


def ratio(inner, square):
    live = square > 0.0
    return jnp.where(live, inner / jnp.where(live, square, 1.0), 0.0)


def total_of(x):
    return jnp.sum(x, keepdims=True)


def share(inner, square, remain):
    lane = lax.broadcasted_iota(jnp.int32, (8, LANES), 1)
    return jnp.where(
        lane == 0, inner, jnp.where(lane == 1, square, jnp.where(lane == 2, remain, 0.0))
    )


def combine(t):
    lane = lax.broadcasted_iota(jnp.int32, t.shape, 1) == 0
    inner = jnp.where(lane, t, 0.0)
    square = jnp.where(lane, pltpu.roll(t, LANES - 1, 1), 0.0)
    remain = jnp.where(lane, pltpu.roll(t, LANES - 2, 1), 0.0)
    inner_sum, square_sum = total_of(inner), total_of(square)
    d = ratio(inner_sum, square_sum) - ratio(inner, square)
    return inner_sum, square_sum, total_of(remain + square * d * d)


def scan_kernel(windows, late, back):
    def tile(r, carry):
        rows = pl.ds(pl.multiple_of(r * 8, 8), 8)
        for c in range(2):
            run = jnp.zeros((8, LANES), jnp.float32)
            sums = [None] * windows
            for v in reversed(range(windows)):
                run = run + late[v, 2 + c, rows, :]
                sums[v] = run
                back[v, c, rows, :] = run
            run = jnp.zeros((8, LANES), jnp.float32)
            for v in range(windows):
                run = run + (late[v, c, rows, :] - late[v, 4 + c, rows, :] * sums[v])
                back[v, 2 + c, rows, :] = run
        return carry

    lax.fori_loop(0, ROWS // 8, tile, 0)


def dots_kernel(back, moved, dual, inc, pm, obs, shares, px, wv, vv, rr):
    windows = back.shape[0]
    per = NF // windows
    rr[...] = jnp.zeros_like(rr)

    def tile(r, carry):
        rows = pl.ds(pl.multiple_of(r * 8, 8), 8)
        total = jnp.zeros((8, LANES), jnp.float32)
        for half in range(2):
            pairs = [(pm[half, rows, :], obs[half, rows, :])]
            for f in range(half * NF // 2, (half + 1) * NF // 2):
                j, c = f // per, f % per
                x = back[j, per + c, rows, :] + moved[f, rows, :]
                px[f, rows, :] = x
                pairs.append((back[j, c, rows, :], dual[f, rows, :]))
                pairs.append((x, inc[f, rows, :]))
            inner = functools.reduce(jnp.add, [p * x for p, x in pairs])
            square = functools.reduce(jnp.add, [x * x for _, x in pairs])
            h = ratio(inner, square)
            for p, x in pairs:
                d = p - h * x
                total = total + d * d
            wv[2 * r + half] = inner
            vv[2 * r + half] = square
        rr[...] += total
        return carry

    lax.fori_loop(0, ROWS // 8, tile, 0)
    inner, square = wv[...], vv[...]
    h = ratio(inner, square)
    inner_sum = total_of(jnp.sum(inner, 0))
    square_sum = total_of(jnp.sum(square, 0))
    d = ratio(inner_sum, square_sum) - h
    remain = total_of(rr[...] + jnp.sum(square * d * d, 0))
    one = share(inner_sum, square_sum, remain)
    for r in range(shares.shape[0] // 8):
        shares[8 * r : 8 * r + 8, :] = one


def final_kernel(
    count, shares, back, px, dual, inc, pm, obs, o_dual, o_obs, o_inc, coeffs, dv, iv, sems
):
    windows = back.shape[0]
    per = NF // windows
    inner, square, remain = combine(shares[...])
    h = inner / square
    scale = jnp.sqrt(remain / count + 1e-06)
    inv = 1.0 / scale
    stores = []
    for n in range(4):
        for f in range(4 * n, 4 * n + 4):
            dv[f] = (back[f // per, f % per] - h * dual[f]) * inv
            iv[f] = (px[f] - h * inc[f]) * inv
        part = slice(4 * n, 4 * n + 4)
        for m, (src, dst) in enumerate(((dv, o_dual), (iv, o_inc))):
            copy = pltpu.make_async_copy(src.at[part], dst.at[part], sems.at[n, m])
            copy.start()
            stores.append(copy)
    first = (lax.broadcasted_iota(jnp.int32, (8, LANES), 0) == 0) & (
        lax.broadcasted_iota(jnp.int32, (8, LANES), 1) == 0
    )
    coeffs[0] = jnp.sum(jnp.where(first, h, 0.0))
    coeffs[1] = jnp.sum(jnp.where(first, scale, 0.0))
    o_obs[...] = (pm[...] - h * obs[...]) * inv
    for copy in stores:
        copy.wait()


def dma(*shape):
    return pltpu.SemaphoreType.DMA(shape)


def block(*shape, at):
    return pl.BlockSpec(shape, lambda i: at)


def across(x, axes):
    return lax.all_to_all(x, axes, 0, 0, tiled=True)


def iteration(dual, obs_dual, increment, trajectory, diffusion, obs_weight, model_var, obs_var):
    windows = lax.axis_size("win")
    columns = lax.axis_size("tx")
    ranks = lax.axis_size("ty")
    devices = windows * columns * ranks
    per = NF // windows
    lam = dual.reshape(NF, ROWS, LANES)
    inc = increment.reshape(NF, ROWS, LANES)
    winds = trajectory.reshape(NW, ROWS, LANES)
    obs = obs_dual.reshape(NO, ROWS, LANES)
    var = model_var.reshape(NF, ROWS, LANES)
    obsvar = obs_var.reshape(NO, ROWS, LANES)
    to_previous = [(i + 1, i) for i in range(windows - 1)]

    every = (lam, inc, winds, obs)
    last = ROWS // 8 - 1
    top, bottom = pl.pallas_call(
        edges_kernel,
        grid=(1,),
        out_shape=(vmem(ALL // 2, 8, LANES), vmem(ALL // 2, 8, LANES)),
        in_specs=[block(x.shape[0], 8, LANES, at=(0, 0, 0)) for x in every]
        + [block(x.shape[0], 8, LANES, at=(0, last, 0)) for x in every],
        out_specs=[VM, VM],
        compiler_params=GRANT,
        name="edges",
    )(*(far(x) for x in every + every))
    south = held(lax.ppermute(bottom, "ty", [(i, i + 1) for i in range(ranks - 1)]))
    north = held(lax.ppermute(top, "ty", [(i + 1, i) for i in range(ranks - 1)]))
    follow = held(lax.ppermute(lam, "win", to_previous))
    packed = pl.pallas_call(
        pack_kernel,
        out_shape=vmem(ROWS, 3 * LANES),
        in_specs=[VM] * 4,
        out_specs=VM,
        compiler_params=GRANT,
        name="pack",
    )(*(held(x) for x in every))
    full = pl.pallas_call(
        edges_halo_kernel,
        out_shape=vmem(EXT, 3 * LANES),
        in_specs=[VM] * 3,
        out_specs=VM,
        compiler_params=GRANT,
        name="edges_halo",
    )(south, north, packed)
    ring = [(i, (i + 1) % columns) for i in range(columns)]
    west = held(lax.ppermute(full, "tx", ring))
    east = held(lax.ppermute(full, "tx", [(j, i) for i, j in ring]))

    fhalo = pl.pallas_call(
        follow_halo_kernel,
        out_shape=vmem(NF + TILES, 8, LANES),
        in_specs=[VM] * 4,
        out_specs=VM,
        compiler_params=GRANT,
        name="follow_halo",
    )(south, north, west, east)
    fhalo = held(lax.ppermute(fhalo, "win", to_previous))

    field = vmem(NF, EXT, 2 * LANES)
    late, moved, pm, wind = pl.pallas_call(
        forward_kernel,
        out_shape=(
            vmem(windows, 3 * per, ROWS, LANES),
            vmem(NF, ROWS, LANES),
            vmem(NO, ROWS, LANES),
            vmem(NW, EXT, 2 * LANES),
        ),
        in_specs=[VM] * 10 + [SM] * 2,
        out_specs=(VM, VM, VM, VM),
        scratch_shapes=[field, field, vmem(NO, ROWS, LANES)],
        compiler_params=GRANT,
        name="forward",
    )(held(inc), held(lam), held(var), held(winds), held(obs), held(obsvar), south, north, west, east, diffusion, obs_weight)
    late = pl.pallas_call(
        adjoint_kernel,
        out_shape=vmem(windows, 3 * per, ROWS, LANES),
        in_specs=[VM] * 10 + [SM] * 2,
        out_specs=VM,
        scratch_shapes=[field, field, vmem(NO, EXT, 2 * LANES)],
        input_output_aliases={0: 0},
        compiler_params=GRANT,
        name="adjoint",
    )(late, held(lam), follow, fhalo, wind, held(obs), south, north, west, east, diffusion, obs_weight)

    late = held(across(late, "win"))
    tiles = 2 * ROWS // 8
    back = pl.pallas_call(
        functools.partial(scan_kernel, windows),
        out_shape=vmem(windows, 2 * per, ROWS, LANES),
        in_specs=[VM],
        out_specs=VM,
        compiler_params=GRANT,
        name="scans",
    )(late)
    back = held(across(back, "win"))
    shares, px = pl.pallas_call(
        dots_kernel,
        out_shape=(vmem(devices, LANES), vmem(NF, ROWS, LANES)),
        in_specs=[VM] * 6,
        out_specs=(VM, VM),
        scratch_shapes=[vmem(tiles, 8, LANES), vmem(tiles, 8, LANES), vmem(8, LANES)],
        compiler_params=GRANT,
        name="dots",
    )(back, moved, held(lam), held(inc), pm, held(obs))
    shares = across(shares, ("win", "tx", "ty"))
    count = float((2 * NF + NO) * ROWS * LANES * devices)
    o_dual, o_obs, o_inc, coeffs = pl.pallas_call(
        functools.partial(final_kernel, count),
        out_shape=(sds(NF, ROWS, LANES), sds(NO, ROWS, LANES), sds(NF, ROWS, LANES), sds(2)),
        in_specs=[VM] * 7,
        out_specs=(HB, VM, HB, SM),
        scratch_shapes=[vmem(NF, ROWS, LANES), vmem(NF, ROWS, LANES), dma(4, 2)],
        compiler_params=GRANT,
        name="final",
    )(held(shares), back, px, held(lam), held(inc), pm, held(obs))
    return (
        o_dual.reshape(dual.shape),
        o_obs.reshape(obs_dual.shape),
        o_inc.reshape(increment.shape),
        coeffs,
    )


def solution(mesh):
    in_specs = (
        P("win", None, None, "ty", "tx"),
        P("win", None, "ty", "tx"),
        P("win", None, None, "ty", "tx"),
        P("win", None, None, None, "ty", "tx"),
        P(),
        P(),
        P("win", None, None, "ty", "tx"),
        P("win", None, "ty", "tx"),
    )
    out_specs = (
        P("win", None, None, "ty", "tx"),
        P("win", None, "ty", "tx"),
        P("win", None, None, "ty", "tx"),
        P(),
    )
    return jax.shard_map(
        iteration, mesh=mesh, in_specs=in_specs, out_specs=out_specs, check_vma=False
    )
```
